768 devices in a mesh: dom: 192 (over y, z, core), sub: 4 (over x).
Axes of the slice: x: 4, y: 8, z: 12, core: 2. Of those that a mesh axis runs over, the one named last changes fastest.
Arguments:
- dof_state: float32 [56, 9, 98304], P(None, None, ('dom', 'sub')), may hold values from -6 to 6
- stiffness: float32 [3, 56, 56], replicated, may hold values from -0.75 to 0.75
- face_proj: float32 [4, 21, 56], replicated, may hold values from -0.75 to 0.75
- face_lift: float32 [4, 56, 21], replicated, may hold values from -1 to 1
- face_rotate: float32 [3, 21, 21], replicated, may hold values from -1.25 to 1.25
- jacobians: float32 [16, 3, 9, 9], replicated, may hold values from -2 to 2
- material: int32 [98304], P(('dom', 'sub')), may hold values from 0 to 15
- inv_jacobian: float32 [3, 3, 98304], P(None, None, ('dom', 'sub')), may hold values from -2.5 to 2.5
- flux_own: float32 [4, 9, 9, 98304], P(None, None, None, ('dom', 'sub')), may hold values from -1.5 to 1.5
- flux_across: float32 [4, 9, 9, 98304], P(None, None, None, ('dom', 'sub')), may hold values from -1.5 to 1.5
- cluster: int32 [98304], P(('dom', 'sub')), may hold values from 0 to 1, as said below
- neighbour: int32 [4, 98304], P(None, ('dom', 'sub')), may hold values from 0 to 224, as said below
- across_face: int32 [4, 98304], P(None, ('dom', 'sub')), may hold values from 0 to 3
- rotation: int32 [4, 98304], P(None, ('dom', 'sub')), may hold values from 0 to 2
- send_list: int32 [73728], P(('dom', 'sub')), may hold values from 0 to 127
Outputs:
- dof_out: float32 [56, 9, 98304], P(None, None, ('dom', 'sub'))
The draws below stay inside these ranges and needn't reach their ends.
Inputs may be any that keep to these rules, and one draw needn't show every extreme that they name: `cluster`: each partition of 128 elements has at most 64 fine elements, and some partition has exactly 64. `neighbour`: values below 128 are the partition's own elements, never the element itself; 128 + g is received slot g; 224 is an outflow face. Every received slot whose source partition exists is named by exactly one face of the partition.
All inputs are finite; a program needn't handle non-finite values.
Results may differ from the reference program's by a relative error of at most 0.0003.
Values sent between devices are 32-bit elements; how exact they have to be, the bound alone decides.
No kernel may reach another device: no remote copies, remote signals or barrier semaphores. Data moves between devices by JAX's collectives and lax.ppermute only.
A program may use at most 64 MiB of HBM per device.

```python
import math
import jax
import jax.numpy as jnp
from jax import lax

NB = 56
NF = 9
FB = 21
ORDER = 6
NMAT = 16
EL = 128
BLK = 8
FINE_MAX = 64
SUBS = 4
SLABS = 192
PARTS_SIZE = 768
GHOSTS = 96
ELEMENTS = 98304


def cluster_ids(key):
    base_key = jax.random.fold_in(key, 101)
    count_key, busy_key, order_key = jax.random.split(base_key, 3)
    raw_counts = jax.random.randint(count_key, (PARTS_SIZE,), 0, FINE_MAX + 1)
    counts = raw_counts * raw_counts // FINE_MAX
    busiest = jax.random.randint(busy_key, (), 0, PARTS_SIZE)
    counts = jnp.where(jnp.arange(PARTS_SIZE) == busiest, FINE_MAX, counts)
    rank_table = jax.vmap(lambda one_key: jax.random.permutation(one_key, EL))(jax.random.split(order_key, PARTS_SIZE))
    labels = jnp.where(rank_table < counts[:, None], 0, 1).astype(jnp.int32)
    return labels.reshape(PARTS_SIZE * EL)


def draw_cluster(key, part):
    return cluster_ids(key)


def draw_inv_jacobian(key, part):
    labels = cluster_ids(key)
    step_scale = jnp.where(labels == 0, 1.0, 0.5).astype(jnp.float32)
    noise_key, factor_key = jax.random.split(jax.random.fold_in(key, 202))
    identity = jnp.eye(3, dtype=jnp.float32)[:, :, None]
    noise = jax.random.truncated_normal(noise_key, -3.0, 3.0, (3, 3, ELEMENTS), jnp.float32)
    factor = jnp.exp(jax.random.uniform(factor_key, (ELEMENTS,), jnp.float32, math.log(0.7), math.log(1.4)))
    return (step_scale * factor)[None, None, :] * (0.5 * identity + 0.35 * noise)


def draw_neighbour(key, part):

    def one_part(part_key, partition):
        local_key, place_key = jax.random.split(part_key)
        slab = partition // SUBS
        sub_pos = partition % SUBS
        slots = jnp.arange(GHOSTS, dtype=jnp.int32)
        peer_slot = slots // BLK
        slab_step = peer_slot // SUBS - 1
        peer_sub = peer_slot % SUBS
        exists = (slab + slab_step >= 0) & (slab + slab_step < SLABS) & jnp.logical_not((slab_step == 0) & (peer_sub == sub_pos))
        outflow = EL + GHOSTS
        ghost_values = jnp.where(exists, EL + slots, outflow)
        face_count = 4 * EL
        positions = jnp.arange(face_count, dtype=jnp.int32)
        owners = positions % EL
        inside = (owners + 1 + jax.random.randint(local_key, (face_count,), 0, EL - 1)) % EL
        placement = jax.random.permutation(place_key, face_count)
        values = jnp.where(placement < GHOSTS, ghost_values[jnp.minimum(placement, GHOSTS - 1)], jnp.where(placement < GHOSTS + EL // 8, outflow, inside))
        return values.reshape(4, EL).astype(jnp.int32)
    part_keys = jax.random.split(jax.random.fold_in(key, 303), PARTS_SIZE)
    every_part = jax.vmap(one_part)(part_keys, jnp.arange(PARTS_SIZE, dtype=jnp.int32))
    return jnp.transpose(every_part, (1, 0, 2)).reshape(4, ELEMENTS)


def place_ends(values, rng, low, largest):
    place = [jax.random.randint(jax.random.fold_in(rng, axis), (), 0, length) for axis, length in enumerate(values.shape)]
    main_axis = values.shape.index(max(values.shape))
    beside = place[:main_axis] + [(place[main_axis] + 1) % values.shape[main_axis]] + place[main_axis + 1:]
    return values.at[tuple(place)].set(low).at[tuple(beside)].set(largest)


def block_scale(rng, dims, cuts, smallest, largest):
    level, own = 1.0, jax.random.fold_in(rng, 6)
    for position, blocks in cuts:
        draws = jnp.exp(jax.random.uniform(jax.random.fold_in(own, position), (blocks,), jnp.float32, smallest / len(cuts), largest / len(cuts)))
        level = level * jnp.repeat(draws, dims[position] // blocks).reshape([-1 if axis == position else 1 for axis in range(len(dims))])
    return level


def normal_values(key, shape, spread, most, cuts=(), held_as=jnp.bfloat16):
    drawn = jax.random.normal(key, shape, jnp.float32) * spread
    if len(cuts) > 0:
        drawn = block_scale(key, shape, cuts, -0.22, 0.18) * drawn
    return jnp.clip(drawn, min=-most, max=most).astype(held_as)


def setup_inputs(seed: int = 0) -> dict:
    key_list = jax.random.split(jax.random.key(seed), 16)
    dof_state = normal_values(key_list[0], (NB, NF, ELEMENTS), 1.0, 6.0, ((2, 768),), jnp.float32)
    stiffness = normal_values(key_list[1], (3, NB, NB), NB ** -0.5, 0.75, (), jnp.float32)
    face_proj = normal_values(key_list[2], (4, FB, NB), NB ** -0.5, 0.75, (), jnp.float32)
    face_lift = normal_values(key_list[3], (4, NB, FB), (2 * FB) ** -0.5, 1.0, (), jnp.float32)
    face_rotate = normal_values(key_list[4], (3, FB, FB), FB ** -0.5, 1.25, (), jnp.float32)
    jacobians = normal_values(key_list[5], (NMAT, 3, NF, NF), NF ** -0.5, 2.0, (), jnp.float32)
    material = place_ends(jax.random.randint(key_list[6], (ELEMENTS,), 0, NMAT), jax.random.fold_in(key_list[6], 1), 0, NMAT - 1).astype(jnp.int32)
    inv_jacobian = draw_inv_jacobian(jax.random.fold_in(key_list[15], 71), 0)
    flux_own = normal_values(key_list[8], (4, NF, NF, ELEMENTS), (2 * NF) ** -0.5, 1.5, ((3, 768),), jnp.float32)
    flux_across = normal_values(key_list[9], (4, NF, NF, ELEMENTS), (2 * NF) ** -0.5, 1.5, ((3, 768),), jnp.float32)
    cluster = draw_cluster(jax.random.fold_in(key_list[15], 71), 0)
    neighbour = draw_neighbour(jax.random.fold_in(key_list[15], 71), 0)
    across_face = place_ends(jax.random.randint(key_list[12], (4, ELEMENTS), 0, 4), jax.random.fold_in(key_list[12], 1), 0, 3).astype(jnp.int32)
    rotation = place_ends(jax.random.randint(key_list[13], (4, ELEMENTS), 0, 3), jax.random.fold_in(key_list[13], 1), 0, 2).astype(jnp.int32)
    send_list = place_ends(jax.random.randint(key_list[14], (PARTS_SIZE * GHOSTS,), 0, EL), jax.random.fold_in(key_list[14], 1), 0, EL - 1).astype(jnp.int32)
    return dict(dof_state=dof_state, stiffness=stiffness, face_proj=face_proj, face_lift=face_lift, face_rotate=face_rotate, jacobians=jacobians, material=material, inv_jacobian=inv_jacobian, flux_own=flux_own, flux_across=flux_across, cluster=cluster, neighbour=neighbour, across_face=across_face, rotation=rotation, send_list=send_list)


HIGH = lax.Precision.HIGHEST


def mix_fields(data, mats):
    return jnp.sum(data[:, :, None, :] * mats[None], axis=1)


def star_of(inv_jacobian, jacobians, material):
    nmat = jacobians.shape[0]
    fields = jacobians.shape[2]
    picked = (material[None, :] == jnp.arange(nmat, dtype=jnp.int32)[:, None]).astype(jnp.float32)
    table = jnp.transpose(jacobians.reshape(nmat, 3 * fields * fields))
    per_elem = jnp.dot(table, picked, precision=HIGH).reshape(3, fields, fields, material.shape[0])
    stacked = []
    for dim_d in range(3):
        summed = inv_jacobian[0, dim_d][None, None, :] * per_elem[0]
        for dim_c in range(1, 3):
            summed = summed + inv_jacobian[dim_c, dim_d][None, None, :] * per_elem[dim_c]
        stacked.append(summed)
    return jnp.stack(stacked)


def derivative(state, stiffness, star_mats):
    total = None
    for dim_d in range(3):
        moved = jnp.einsum('xb,xqe->bqe', stiffness[dim_d], state, precision=HIGH)
        term = mix_fields(moved, star_mats[dim_d])
        total = term if total is None else total + term
    return -total


def taylor(state, stiffness, star_mats):
    series = [state]
    for order in range(ORDER - 1):
        series.append(derivative(series[-1], stiffness, star_mats))
    return series


def integral(series, start_time, end_time):
    summed = jnp.zeros_like(series[0])
    for order in range(len(series)):
        factor = (end_time ** (order + 1) - start_time ** (order + 1)) / math.factorial(order + 1)
        summed = summed + factor * series[order]
    return summed


def volume(own_integral, stiffness, star_mats):
    total = None
    for dim_d in range(3):
        weighted = mix_fields(own_integral, star_mats[dim_d])
        term = jnp.einsum('bx,xpe->bpe', stiffness[dim_d], weighted, precision=HIGH)
        total = term if total is None else total + term
    return total


def lift_faces(solved_list, face_lift):
    faces, basis, face_basis = face_lift.shape
    lifter = jnp.transpose(face_lift, (1, 0, 2)).reshape(basis, faces * face_basis)
    return jnp.einsum('bg,gpe->bpe', lifter, jnp.concatenate(solved_list, axis=0), precision=HIGH)


def local_faces(own_integral, face_proj, face_lift, flux_own):
    faces, face_basis, basis = face_proj.shape
    projected = jnp.einsum('gx,xqe->gqe', face_proj.reshape(faces * face_basis, basis), own_integral, precision=HIGH)
    solved_list = [mix_fields(projected[i * face_basis:(i + 1) * face_basis], flux_own[i]) for i in range(faces)]
    return lift_faces(solved_list, face_lift)


def neighbour_faces(near_list, across_face, rotation, face_proj, face_lift, face_rotate, flux_across):
    faces, face_basis, basis = face_proj.shape
    combos = jnp.einsum('hfg,jgx->hjfx', face_rotate, face_proj, precision=HIGH).reshape(12 * face_basis, basis)
    solved_list = []
    for i in range(faces):
        near = near_list[i]
        projected = jnp.einsum('gx,xqe->gqe', combos, near, precision=HIGH)
        projected = projected.reshape(12, face_basis, near.shape[1], near.shape[2])
        choice_key = rotation[i] * 4 + across_face[i]
        pick = (choice_key[None, :] == jnp.arange(12, dtype=jnp.int32)[:, None]).astype(jnp.float32)
        chosen = jnp.sum(projected * pick[:, None, None, :], axis=0)
        solved_list.append(mix_fields(chosen, flux_across[i]))
    return lift_faces(solved_list, face_lift)


def update(base_state, own_integral, near_list, stiffness, star_mats, face_proj, face_lift, face_rotate,
           flux_own, flux_across, across_face, rotation):
    result = base_state + volume(own_integral, stiffness, star_mats)
    result = result - local_faces(own_integral, face_proj, face_lift, flux_own)
    return result - neighbour_faces(near_list, across_face, rotation, face_proj, face_lift, face_rotate, flux_across)


def neighbour_sources(neighbour, send_list):
    partition = jnp.arange(PARTS_SIZE, dtype=jnp.int32)[:, None]
    slots = jnp.arange(GHOSTS, dtype=jnp.int32)[None, :]
    peer_slot = slots // BLK
    member = slots % BLK
    slab_step = peer_slot // SUBS - 1
    peer_sub = peer_slot % SUBS
    slab = partition // SUBS
    sub_pos = partition % SUBS
    exists = (slab + slab_step >= 0) & (slab + slab_step < SLABS) & jnp.logical_not((slab_step == 0) & (peer_sub == sub_pos))
    peer = jnp.clip((slab + slab_step) * SUBS + peer_sub, 0, PARTS_SIZE - 1)
    back_block = (1 - slab_step) * SUBS + sub_pos
    listed = send_list[peer * GHOSTS + back_block * BLK + member]
    ghost_src = jnp.where(exists, peer * EL + listed, ELEMENTS).astype(jnp.int32)
    owners = jnp.broadcast_to((jnp.arange(ELEMENTS, dtype=jnp.int32) // EL)[None, :], neighbour.shape)
    ghost_pick = ghost_src[owners, jnp.clip(neighbour - EL, 0, GHOSTS - 1)]
    inside = neighbour < EL
    received = (neighbour >= EL) & (neighbour < EL + GHOSTS)
    return jnp.where(inside, owners * EL + neighbour, jnp.where(received, ghost_pick, ELEMENTS)).astype(jnp.int32)


def to_blocks(array):
    lead = array.shape[:-1]
    return jnp.moveaxis(array.reshape(lead + (SLABS, SUBS * EL)), -2, 0)


def from_blocks(array):
    moved_back = jnp.moveaxis(array, 0, -2)
    return moved_back.reshape(moved_back.shape[:-2] + (ELEMENTS,))


def reference(dof_state, stiffness, face_proj, face_lift, face_rotate, jacobians, material, inv_jacobian,
              flux_own, flux_across, cluster, neighbour, across_face, rotation, send_list):
    sources = neighbour_sources(neighbour, send_list)
    state_blocks = to_blocks(dof_state)
    inv_blocks = to_blocks(inv_jacobian)
    mat_blocks = to_blocks(material)
    own_blocks = to_blocks(flux_own)
    across_blocks = to_blocks(flux_across)
    source_blocks = to_blocks(sources)
    face_blocks = to_blocks(across_face)
    turn_blocks = to_blocks(rotation)
    cluster_blocks = to_blocks(cluster)
    zero_column = jnp.zeros((NB, NF, 1), dof_state.dtype)

    def predict_block(pieces):
        state_block, inv_block, mat_block = pieces
        star_mats = star_of(inv_block, jacobians, mat_block)
        series = taylor(state_block, stiffness, star_mats)
        return integral(series, 0.0, 1.0), integral(series, 1.0, 2.0)

    first_blocks, second_blocks = lax.map(predict_block, (state_blocks, inv_blocks, mat_blocks))
    padded_first = jnp.concatenate([from_blocks(first_blocks), zero_column], axis=2)

    def fine_block(pieces):
        (state_block, first_block, second_block, inv_block, mat_block, own_block, across_block,
         source_block, face_block, turn_block, cluster_block) = pieces
        star_mats = star_of(inv_block, jacobians, mat_block)
        near_list = [jnp.take(padded_first, source_block[i], axis=2) for i in range(4)]
        stepped = update(state_block, first_block, near_list, stiffness, star_mats, face_proj, face_lift,
                         face_rotate, own_block, across_block, face_block, turn_block)
        second_step = integral(taylor(stepped, stiffness, star_mats), 0.0, 1.0)
        is_fine = cluster_block == 0
        later_half = jnp.where(is_fine, second_step, second_block)
        base_state = jnp.where(is_fine, stepped, state_block)
        own_integral = jnp.where(is_fine, second_step, first_block + second_block)
        return later_half, base_state, own_integral

    later_blocks, base_blocks, integral_blocks = lax.map(
        fine_block, (state_blocks, first_blocks, second_blocks, inv_blocks, mat_blocks, own_blocks,
                     across_blocks, source_blocks, face_blocks, turn_blocks, cluster_blocks))
    padded_later = jnp.concatenate([from_blocks(later_blocks), zero_column], axis=2)

    def final_block(pieces):
        (base_block, integral_block, inv_block, mat_block, own_block, across_block, source_block,
         face_block, turn_block, cluster_block) = pieces
        star_mats = star_of(inv_block, jacobians, mat_block)
        is_fine = (cluster_block == 0)[None, None, :]
        near_list = []
        for i in range(4):
            near_first = jnp.take(padded_first, source_block[i], axis=2)
            near_later = jnp.take(padded_later, source_block[i], axis=2)
            near_list.append(jnp.where(is_fine, near_later, near_first + near_later))
        return update(base_block, integral_block, near_list, stiffness, star_mats, face_proj, face_lift,
                      face_rotate, own_block, across_block, face_block, turn_block)

    out_blocks = lax.map(final_block, (base_blocks, integral_blocks, inv_blocks, mat_blocks, own_blocks,
                                       across_blocks, source_blocks, face_blocks, turn_blocks, cluster_blocks))
    return from_blocks(out_blocks)
```

```python
import math

import jax
import jax.numpy as jnp
from jax import lax
from jax.experimental import pallas as pl
from jax.experimental.pallas import tpu as pltpu
from jax.sharding import PartitionSpec as P

ORDER = 6
NB, NF, FB, EL = 56, 9, 21, 128
FP = 24
WID = NF * EL
HIGH = lax.Precision.HIGHEST
F32 = jnp.float32
BF16 = jnp.bfloat16
AXES = ("dom", "sub")


def dot32(a, b):
    return jnp.dot(a, b, preferred_element_type=F32)


def halves(x):
    hi = x.astype(BF16)
    return hi, (x - hi.astype(F32)).astype(BF16)


def put_rhs(rhs, cols, x):
    hi, lo = halves(jnp.concatenate([x, jnp.zeros((8, x.shape[1]), F32)], axis=0))
    rhs[0:64, cols] = hi
    rhs[64:128, cols] = lo
    rhs[128:192, cols] = hi


def put_lhs(lhs, rows, a):
    hi, lo = halves(a)
    lhs[rows, 0:NB] = hi
    lhs[rows, 64 : 64 + NB] = hi
    lhs[rows, 128 : 128 + NB] = lo


def field(p):
    return slice(p * EL, (p + 1) * EL)


PAIRS = ((0, 1), (2, 3), (4, 5), (6, 7), (8,))


def pair_cols(group):
    return slice(group[0] * EL, (group[-1] + 1) * EL)


def mix_star(moved, star, group):
    acc = [None] * len(group)
    for d in range(3):
        for q in range(NF):
            m = moved[d * NB : (d + 1) * NB, field(q)].reshape(7, 8, EL)
            for n, p in enumerate(group):
                t = m * star[pl.ds(d * 81 + q * 9 + p, 8, stride=0), :][None]
                acc[n] = t if acc[n] is None else acc[n] + t
    return [a.reshape(NB, EL) for a in acc]


def run_series(lhs, rhs, moved, star, add):
    for group in PAIRS:
        cols = pair_cols(group)
        moved[0, :, cols] = dot32(lhs[...], rhs[:, cols])
    for order in range(1, ORDER):
        src = moved.at[(order - 1) % 2]
        for group in PAIRS:
            cols = pair_cols(group)
            for p, block in zip(group, mix_star(src, star, group)):
                add(order, p, block)
                if order < ORDER - 1:
                    put_rhs(rhs, field(p), block)
            if order < ORDER - 1:
                moved[order % 2, :, cols] = dot32(lhs[...], rhs[:, cols])


def pack_blocks(ids, send, payload, gat, res, trans, other, main):
    slots = jnp.concatenate([send[...], jnp.full((1, EL - send.shape[1]), -1, jnp.int32)], axis=1)
    rows = lax.broadcasted_iota(jnp.int32, (EL, EL), 0)
    pick = jnp.where(rows == slots, 1.0, 0.0).astype(BF16)
    pick = jnp.concatenate([pick, pick], axis=0)
    for q in range(NF):
        x = jnp.concatenate([payload[:, field(q)], jnp.zeros((8, EL), F32)], axis=0)
        hi, lo = halves(x)
        gat[q * 64 : (q + 1) * 64, 0:EL] = hi
        gat[q * 64 : (q + 1) * 64, EL : 2 * EL] = lo
    got = dot32(gat[...], pick)
    for q in range(NF):
        res[q * NB : (q + 1) * NB, :] = got[q * 64 : q * 64 + NB]
    res[NF * NB : 512, :] = jnp.zeros((8, EL), F32)
    trans[...] = res[...].T
    core = ids[0]
    for r in range(4):
        other[r] = trans[pl.ds(pl.multiple_of(8 * (2 * core * 4 + r), 8), 8), :]
    for c in range(2):
        for r in range(4):
            main[c * 4 + r] = trans[pl.ds(pl.multiple_of(8 * ((c - core + 1) * 4 + r), 8), 8), :]


def k_predict(ids, dof, stiff, jac, mat, inv, send, star, first, second, other, main, lhs_out, lhs, rhs, moved, gat, res, trans):
    pick = (lax.broadcasted_iota(jnp.int32, (16, EL), 0) == mat[...]).astype(F32)
    per = [jnp.dot(jac[:, c, :], pick, precision=HIGH, preferred_element_type=F32) for c in range(3)]
    for d in range(3):
        total = None
        for c in range(3):
            t = per[c] * inv[c, pl.ds(d, 1), :]
            total = t if total is None else total + t
        star[d * 81 : (d + 1) * 81, :] = total
    lhs[...] = jnp.zeros(lhs.shape, BF16)
    for d in range(3):
        put_lhs(lhs, slice(d * NB, (d + 1) * NB), -(stiff[d].T))
    lhs_out[...] = lhs[...]
    for p in range(NF):
        x = dof[p]
        put_rhs(rhs, field(p), x)
        first[:, field(p)] = x
        second[:, field(p)] = x

    def add(order, p, block):
        scale = 1.0 / math.factorial(order + 1)
        first[:, field(p)] = first[:, field(p)] + scale * block
        second[:, field(p)] = second[:, field(p)] + ((2 ** (order + 1) - 1) * scale) * block

    run_series(lhs, rhs, moved, star, add)
    pack_blocks(ids, send, first, gat, res, trans, other, main)


def face_mix(source, flux, face, p, lane):
    acc = None
    for q in range(NF):
        t = source(q).reshape(3, 8, EL) * jnp.broadcast_to(flux[q * 9 + p, pl.ds(face, 1), :], (8, EL))[None]
        acc = t if acc is None else acc + t
    return acc.reshape(FP, EL)


def own_terms(both, rhs, moved, star, flux_own, lift_own, solved, put):
    for group in PAIRS:
        cols = pair_cols(group)
        moved[:, cols] = dot32(both[...], rhs[:, cols])
    for p in range(NF):
        for i in range(4):
            base = 3 * NB + i * FP
            s = face_mix(lambda q: moved[base : base + FP, field(q)], flux_own, i, p, EL)
            solved[i * FP : (i + 1) * FP, field(p)] = s
    for group in PAIRS:
        cols = pair_cols(group)
        hi, lo = halves(solved[:, cols])
        lifted = dot32(lift_own[0], hi) + dot32(lift_own[0], lo) + dot32(lift_own[1], hi)
        for n, (p, block) in enumerate(zip(group, mix_star(moved, star, group))):
            put(p, block + lifted[:, n * EL : (n + 1) * EL])


def gather_table(source, table):
    for q in range(NF):
        for j in range(4):
            table[q * FP : (q + 1) * FP, j * EL : (j + 1) * EL] = source(j, q)
    table[NF * FP : 224, :] = jnp.zeros((8, 4 * EL), F32)


def gather_from(table, hot):
    hi, lo = halves(table[...])
    return dot32(hi, hot) + dot32(lo, hot)


def k_window_a(first, dof, star, stiff, proj, lift, rotate, flux_own, nbr, across,
               base, chosen, hot_own, hot_ghost, both, lift_own, lift_rot,
               rhs, moved, solved, table, lift_f, rot_f):
    both[...] = jnp.zeros(both.shape, BF16)
    for d in range(3):
        put_lhs(both, slice(d * NB, (d + 1) * NB), stiff[d])
    for j in range(4):
        a = jnp.concatenate([proj[:, j, :], jnp.zeros((3, NB), F32)], axis=0)
        put_lhs(both, slice(3 * NB + j * FP, 3 * NB + (j + 1) * FP), a)
    lift_f[...] = jnp.zeros(lift_f.shape, F32)
    rot_f[...] = jnp.zeros(rot_f.shape, F32)
    for i in range(4):
        a = -lift[:, i, :]
        lift_f[i * FP : i * FP + FB, :] = a
        for h in range(3):
            turned = lax.dot_general(rotate[h], a, (((0,), (0,)), ((), ())), precision=HIGH, preferred_element_type=F32)
            rot_f[h * 96 + i * FP : h * 96 + i * FP + FB, :] = turned
    lo_hi, lo_lo = halves(lift_f[...].T)
    lift_own[0] = lo_hi
    lift_own[1] = lo_lo
    lr_hi, lr_lo = halves(rot_f[...].T)
    lift_rot[0:NB] = lr_hi
    lift_rot[NB : 2 * NB] = lr_lo
    rows = lax.broadcasted_iota(jnp.int32, (EL, EL), 0)
    for i in range(4):
        n = nbr[pl.ds(i, 1), :]
        key = across[pl.ds(i, 1), :] * EL + jnp.where(n < EL, n, n + (3 * EL))
        for j in range(4):
            hot_own[j * EL : (j + 1) * EL, field(i)] = jnp.where(rows + j * EL == key, 1.0, 0.0).astype(BF16)
            hot_ghost[j * EL : (j + 1) * EL, field(i)] = jnp.where(rows + (j + 4) * EL == key, 1.0, 0.0).astype(BF16)
    for p in range(NF):
        put_rhs(rhs, field(p), first[:, field(p)])

    def put(p, block):
        base[:, field(p)] = dof[p] + block

    own_terms(both, rhs, moved, star, flux_own, lift_own, solved, put)
    gather_table(lambda j, q: moved[3 * NB + j * FP : 3 * NB + (j + 1) * FP, field(q)], table)
    chosen[...] = gather_from(table, hot_own[...])


def k_window_b(later, own, part, star, flux_own, hot_own, both, lift_own,
               base, chosen, rhs, moved, solved, table, proj_b):
    for p in range(NF):
        put_rhs(rhs, field(p), later[:, field(p)])
    for group in PAIRS:
        cols = pair_cols(group)
        proj_b[:, cols] = dot32(both[3 * NB :, :], rhs[:, cols])
    gather_table(lambda j, q: proj_b[j * FP : (j + 1) * FP, field(q)], table)
    chosen[...] = gather_from(table, hot_own[...])
    for p in range(NF):
        put_rhs(rhs, field(p), own[:, field(p)])

    def put(p, block):
        base[:, field(p)] = part[:, field(p)] + block

    own_terms(both, rhs, moved, star, flux_own, lift_own, solved, put)


def near_terms(ids, recv, chosen, hot_ghost, both, lift_rot, flux_across, rot,
               ghost, ghost_t, rhs, proj_g, table, near, solved, turned, put):
    core = ids[0]
    pos = ids[1]
    for s in range(4):
        keep = jnp.where(pos == s, 0.0, 1.0).astype(F32)
        ghost[(4 + s) * 8 : (5 + s) * 8, :] = recv[0, core * 4 + s] * keep
        row = pl.multiple_of(8 * ((2 - 2 * core) * 4 + s), 8)
        ghost[pl.ds(row, 8), :] = recv[0, (1 - core) * 4 + s]
        row = pl.multiple_of(8 * (2 * core * 4 + s), 8)
        ghost[pl.ds(row, 8), :] = recv[1, core * 4 + s]
    ghost[96:EL, :] = jnp.zeros((EL - 96, 512), F32)
    ghost_t[...] = ghost[...].T
    for q in range(NF):
        put_rhs(rhs, field(q), ghost_t[q * NB : (q + 1) * NB, :])
    for group in PAIRS:
        cols = pair_cols(group)
        proj_g[:, cols] = dot32(both[3 * NB :, :], rhs[:, cols])
    gather_table(lambda j, q: proj_g[j * FP : (j + 1) * FP, field(q)], table)
    near[...] = chosen[...] + gather_from(table, hot_ghost[...])
    for p in range(NF):
        for i in range(4):
            s = face_mix(lambda q: near[q * FP : (q + 1) * FP, field(i)], flux_across, i, p, EL)
            solved[i * FP : (i + 1) * FP, field(p)] = s
    masks = []
    for h in range(3):
        m = [jnp.broadcast_to(jnp.where(rot[pl.ds(i, 1), :] == h, 1.0, 0.0), (FP, EL)) for i in range(4)]
        masks.append(jnp.concatenate(m, axis=0).astype(BF16))
    for group in PAIRS:
        for p in group:
            hi, lo = halves(solved[:, field(p)])
            for h in range(3):
                turned[0, h * 96 : (h + 1) * 96, field(p)] = hi * masks[h]
                turned[1, h * 96 : (h + 1) * 96, field(p)] = lo * masks[h]
        cols = pair_cols(group)
        top = dot32(lift_rot[...], turned[0, :, cols])
        put(group, top[0:NB] + top[NB : 2 * NB] + dot32(lift_rot[0:NB, :], turned[1, :, cols]))


def k_middle(ids, recv, chosen, hot_ghost, both, lift_rot, flux_across, rot, base, lhs, star, first, second, dof, cluster, send,
             later, own, part, other, main,
             ghost, ghost_t, rhs, proj_g, table, near, solved, turned, moved, total, gat, res):
    fine = cluster[...] == 0

    def put(group, block):
        for n, p in enumerate(group):
            b = block[:, n * EL : (n + 1) * EL]
            stepped = base[:, field(p)] + b
            part[:, field(p)] = jnp.where(fine, stepped, dof[p] + b)
            total[:, field(p)] = stepped
            put_rhs(rhs, field(p), stepped)

    near_terms(ids, recv, chosen, hot_ghost, both, lift_rot, flux_across, rot,
               ghost, ghost_t, rhs, proj_g, table, near, solved, turned, put)

    def add(order, p, block):
        scale = 1.0 / math.factorial(order + 1)
        t = total[:, field(p)] + scale * block
        if order < ORDER - 1:
            total[:, field(p)] = t
        else:
            sec = second[:, field(p)]
            later[:, field(p)] = jnp.where(fine, t, sec)
            own[:, field(p)] = jnp.where(fine, t, first[:, field(p)] + sec)

    run_series(lhs, rhs, moved, star, add)
    pack_blocks(ids, send, later, gat, res, ghost, other, main)


def k_final(ids, recv, chosen, hot_ghost, both, lift_rot, flux_across, rot, base, out,
            ghost, ghost_t, rhs, proj_g, table, near, solved, turned):
    def put(group, block):
        for n, p in enumerate(group):
            out[p] = base[:, field(p)] + block[:, n * EL : (n + 1) * EL]

    near_terms(ids, recv, chosen, hot_ghost, both, lift_rot, flux_across, rot,
               ghost, ghost_t, rhs, proj_g, table, near, solved, turned, put)


def call(kernel, name, outs, scratch, smem_first, *args):
    space = [pl.BlockSpec(memory_space=pltpu.VMEM) for _ in args]
    if smem_first:
        space[0] = pl.BlockSpec(memory_space=pltpu.SMEM)
    return pl.pallas_call(
        kernel,
        out_shape=[jax.ShapeDtypeStruct(s, d) for s, d in outs],
        in_specs=space,
        out_specs=[pl.BlockSpec(memory_space=pltpu.VMEM) for _ in outs],
        scratch_shapes=[pltpu.VMEM(s, d) for s, d in scratch],
        name=name,
    )(*args)


def exchange_start(other, slabs):
    pairs = []
    for a in range(1, slabs - 1, 2):
        for s in range(4):
            pairs += [(a * 4 + s, (a + 1) * 4 + s), ((a + 1) * 4 + s, a * 4 + s)]
    return lax.ppermute(other, AXES, pairs)


def exchange_end(relay, main, slabs):
    groups = [[(2 * c + b) * 4 + s for b in range(2) for s in range(4)] for c in range(slabs // 2)]
    message = jnp.stack([main, jnp.concatenate([relay, relay], axis=0)])
    return lax.all_to_all(message, AXES, 1, 1, axis_index_groups=groups)


def local(dof_state, stiffness, face_proj, face_lift, face_rotate, jacobians, material, inv_jacobian,
          flux_own, flux_across, cluster, neighbour, across_face, rotation, send_list):
    slabs = lax.axis_size("dom")
    ids = jnp.stack([lax.axis_index("dom") % 2, lax.axis_index("sub")]).astype(jnp.int32)
    dof = jnp.transpose(dof_state, (1, 0, 2))
    jac = jnp.transpose(jacobians, (2, 3, 1, 0)).reshape(81, 3, 16)
    proj = jnp.transpose(face_proj, (1, 0, 2))
    lift = jnp.transpose(face_lift, (2, 0, 1))
    f_own = jnp.transpose(flux_own, (1, 2, 0, 3)).reshape(81, 4, EL)
    f_across = jnp.transpose(flux_across, (1, 2, 0, 3)).reshape(81, 4, EL)
    mat = material.reshape(1, EL)
    clu = cluster.reshape(1, EL)
    send = send_list.reshape(1, 96)
    state = ((NB, WID), F32)
    blocks = [((4, 8, 512), F32), ((8, 8, 512), F32)]
    rhs = ((192, WID), BF16)
    pack = [((576, 2 * EL), BF16), ((512, EL), F32), ((EL, 512), F32)]
    star, first, second, other, main, lhs = call(
        k_predict, "predict", [((243, EL), F32), state, state, *blocks, ((168, 192), BF16)],
        [((168, 192), BF16), rhs, ((2, 168, WID), F32), *pack],
        True, ids, dof, stiffness, jac, mat, inv_jacobian, send)
    relay = exchange_start(other, slabs)
    table = ((224, 512), F32)
    hot = ((512, 512), BF16)
    base, chosen, hot_own, hot_ghost, both, lift_own, lift_rot = call(
        k_window_a, "window_a",
        [state, table, hot, hot, ((264, 192), BF16), ((2, NB, 96), BF16), ((2 * NB, 288), BF16)],
        [rhs, ((264, WID), F32), ((96, WID), F32), table, ((96, NB), F32), ((288, NB), F32)],
        False, first, dof, star, stiffness, proj, lift, face_rotate, f_own, neighbour, across_face)
    recv = exchange_end(relay, main, slabs)
    near_scratch = [((EL, 512), F32), ((512, EL), F32), rhs, ((96, WID), F32), table, table, ((96, WID), F32), ((2, 288, WID), BF16)]
    later, own, part, other, main = call(
        k_middle, "middle", [state, state, state, *blocks],
        [*near_scratch, ((2, 168, WID), F32), state, pack[0], pack[1]],
        True, ids, recv, chosen, hot_ghost, both, lift_rot, f_across, rotation, base, lhs, star, first, second, dof, clu, send)
    relay = exchange_start(other, slabs)
    base, chosen = call(
        k_window_b, "window_b", [state, table],
        [rhs, ((264, WID), F32), ((96, WID), F32), table, ((96, WID), F32)],
        False, later, own, part, star, f_own, hot_own, both, lift_own)
    recv = exchange_end(relay, main, slabs)
    (out,) = call(
        k_final, "final", [((NF, NB, EL), F32)], near_scratch,
        True, ids, recv, chosen, hot_ghost, both, lift_rot, f_across, rotation, base)
    return jnp.transpose(out, (1, 0, 2))


def solution(mesh):
    both = ("dom", "sub")
    in_specs = (
        P(None, None, both), P(), P(), P(), P(), P(), P(both), P(None, None, both),
        P(None, None, None, both), P(None, None, None, both), P(both), P(None, both),
        P(None, both), P(None, both), P(both),
    )
    return jax.shard_map(local, mesh=mesh, in_specs=in_specs, out_specs=P(None, None, both), check_vma=False)
```

```python
import math

import jax
import jax.numpy as jnp
from jax import lax
from jax.experimental import pallas as pl
from jax.experimental.pallas import tpu as pltpu
from jax.sharding import PartitionSpec as P

ORDER = 6
NB, NF, FB, EL = 56, 9, 21, 128
FP = 24
WID = NF * EL
HIGH = lax.Precision.HIGHEST
F32 = jnp.float32
BF16 = jnp.bfloat16
AXES = ("dom", "sub")


def dot32(a, b):
    return jnp.dot(a, b, preferred_element_type=F32)


def halves(x):
    hi = x.astype(BF16)
    return hi, (x - hi.astype(F32)).astype(BF16)


def put_rhs(rhs, cols, x):
    hi, lo = halves(jnp.concatenate([x, jnp.zeros((8, x.shape[1]), F32)], axis=0))
    rhs[0:64, cols] = hi
    rhs[64:128, cols] = lo
    rhs[128:192, cols] = hi


def put_lhs(lhs, rows, a):
    hi, lo = halves(a)
    lhs[rows, 0:NB] = hi
    lhs[rows, 64 : 64 + NB] = hi
    lhs[rows, 128 : 128 + NB] = lo


def field(p):
    return slice(p * EL, (p + 1) * EL)


PAIRS = ((0, 1), (2, 3), (4, 5), (6, 7), (8,))


def pair_cols(group):
    return slice(group[0] * EL, (group[-1] + 1) * EL)


def mix_star(moved, star, group):
    acc = [None] * len(group)
    for d in range(3):
        for q in range(NF):
            m = moved[d * NB : (d + 1) * NB, field(q)].reshape(7, 8, EL)
            for n, p in enumerate(group):
                t = m * star[pl.ds(d * 81 + q * 9 + p, 8, stride=0), :][None]
                acc[n] = t if acc[n] is None else acc[n] + t
    return [a.reshape(NB, EL) for a in acc]


def run_series(lhs, rhs, moved, star, add):
    for group in PAIRS:
        cols = pair_cols(group)
        moved[0, :, cols] = dot32(lhs[...], rhs[:, cols])
    for order in range(1, ORDER):
        src = moved.at[(order - 1) % 2]
        for group in PAIRS:
            cols = pair_cols(group)
            for p, block in zip(group, mix_star(src, star, group)):
                add(order, p, block)
                if order < ORDER - 1:
                    put_rhs(rhs, field(p), block)
            if order < ORDER - 1:
                moved[order % 2, :, cols] = dot32(lhs[...], rhs[:, cols])


def send_slots(send):
    return jnp.concatenate([send[...], jnp.full((1, EL - send.shape[1]), -1, jnp.int32)], axis=1)


def pack_blocks(slots, payload, gat, res, trans, other, main):
    rows = lax.broadcasted_iota(jnp.int32, (EL, EL), 0)
    pick = jnp.where(rows == slots, 1.0, 0.0).astype(BF16)
    pick = jnp.concatenate([pick, pick], axis=0)
    for q in range(NF):
        x = jnp.concatenate([payload[:, field(q)], jnp.zeros((8, EL), F32)], axis=0)
        hi, lo = halves(x)
        gat[q * 64 : (q + 1) * 64, 0:EL] = hi
        gat[q * 64 : (q + 1) * 64, EL : 2 * EL] = lo
    got = dot32(gat[...], pick)
    for q in range(NF):
        res[q * NB : (q + 1) * NB, :] = got[q * 64 : q * 64 + NB]
    res[NF * NB : 512, :] = jnp.zeros((8, EL), F32)
    trans[...] = res[...].T
    core = lax.axis_index("dom") % 2
    for r in range(4):
        other[r] = trans[pl.ds(pl.multiple_of(8 * (2 * core * 4 + r), 8), 8), :]
    for c in range(2):
        for r in range(4):
            main[c * 4 + r] = trans[pl.ds(pl.multiple_of(8 * ((c - core + 1) * 4 + r), 8), 8), :]


def k_predict(mat, jac, inv, stiff, dof, send, star, first, second, other, main, lhs_out, lhs, rhs, moved, gat, res, trans):
    mat, jac, inv = mat.ready(), jac.ready(), inv.ready()
    star_out, first_out, second_out = star, first, second
    star, first, second = star.ref, first.ref, second.ref
    pick = (lax.broadcasted_iota(jnp.int32, (16, EL), 0) == mat[...]).astype(F32)
    per = [jnp.dot(jac[:, c, :], pick, precision=HIGH, preferred_element_type=F32) for c in range(3)]
    for d in range(3):
        total = None
        for c in range(3):
            t = per[c] * inv[c, pl.ds(d, 1), :]
            total = t if total is None else total + t
        star[d * 81 : (d + 1) * 81, :] = total
    star_out.flush()
    stiff = stiff.ready()
    lhs[...] = jnp.zeros(lhs.shape, BF16)
    for d in range(3):
        put_lhs(lhs, slice(d * NB, (d + 1) * NB), -(stiff[d].T))
    lhs_out.ref[...] = lhs[...]
    lhs_out.flush()
    dof = dof.ready()
    for p in range(NF):
        x = dof[p]
        put_rhs(rhs, field(p), x)
        first[:, field(p)] = x
        second[:, field(p)] = x

    def add(order, p, block):
        scale = 1.0 / math.factorial(order + 1)
        first[:, field(p)] = first[:, field(p)] + scale * block
        second[:, field(p)] = second[:, field(p)] + ((2 ** (order + 1) - 1) * scale) * block

    run_series(lhs, rhs, moved, star, add)
    first_out.flush()
    second_out.flush()
    pack_blocks(send_slots(send.ready()), first, gat, res, trans, other.ref, main.ref)


def face_mix(source, flux, face, p, lane):
    acc = None
    for q in range(NF):
        t = source(q).reshape(3, 8, EL) * jnp.broadcast_to(flux[q * 9 + p, pl.ds(face, 1), :], (8, EL))[None]
        acc = t if acc is None else acc + t
    return acc.reshape(FP, EL)


def own_terms(both, rhs, moved, star, flux_own, lift_own, solved, put):
    for group in PAIRS:
        cols = pair_cols(group)
        moved[:, cols] = dot32(both[...], rhs[:, cols])
    for p in range(NF):
        for i in range(4):
            base = 3 * NB + i * FP
            s = face_mix(lambda q: moved[base : base + FP, field(q)], flux_own, i, p, EL)
            solved[i * FP : (i + 1) * FP, field(p)] = s
    for group in PAIRS:
        cols = pair_cols(group)
        hi, lo = halves(solved[:, cols])
        lifted = dot32(lift_own[0], hi) + dot32(lift_own[0], lo) + dot32(lift_own[1], hi)
        for n, (p, block) in enumerate(zip(group, mix_star(moved, star, group))):
            put(p, block + lifted[:, n * EL : (n + 1) * EL])


def gather_table(source, table, table_f):
    for q in range(NF):
        for j in range(4):
            table_f[q * FP : (q + 1) * FP, j * EL : (j + 1) * EL] = source(j, q)
    table_f[NF * FP : 224, :] = jnp.zeros((8, 4 * EL), F32)
    hi, lo = halves(table_f[...])
    table[0:224, :] = hi
    table[224:448, :] = lo


def gather_from(table, hot):
    got = dot32(table[...], hot)
    return got[0:224] + got[224:448]


class Window:
    def __init__(self, ref, start, stop, width):
        self.ref, self.start, self.stop, self.width = ref, start, stop, width
        self.shape = (stop - start, width)

    def place(self, key):
        key = key if isinstance(key, tuple) else (key,)
        rows = slice(None) if key[0] is Ellipsis else key[0]
        cols = key[1] if len(key) > 1 else slice(None)
        first, last, _ = rows.indices(self.stop - self.start)
        left, right, _ = cols.indices(self.width)
        return slice(self.start + first, self.start + last), slice(left, right)

    def __getitem__(self, key):
        return self.ref[self.place(key)]

    def __setitem__(self, key, value):
        self.ref[self.place(key)] = value


def weight_parts(weights):
    return Window(weights, 0, 264, 192), Window(weights, 264, 432, 192), Window(weights, 432, 544, 288)


def k_own_a(stiff, proj, lift, rotate, first, flux_own, star, dof, lhs, second,
            state, projected, weights, lift_own, rhs, moved, solved, lift_f, rot_f):
    stiff, proj, lift, rotate = stiff.ready(), proj.ready(), lift.ready(), rotate.ready()
    state, projected, lift_own = state.ref, projected.ref, lift_own.ref
    both, lhs_out, lift_rot = weight_parts(weights.ref)
    both[...] = jnp.zeros(both.shape, BF16)
    for d in range(3):
        put_lhs(both, slice(d * NB, (d + 1) * NB), stiff[d])
    for j in range(4):
        a = jnp.concatenate([proj[:, j, :], jnp.zeros((3, NB), F32)], axis=0)
        put_lhs(both, slice(3 * NB + j * FP, 3 * NB + (j + 1) * FP), a)
    lift_f[...] = jnp.zeros(lift_f.shape, F32)
    rot_f[...] = jnp.zeros(rot_f.shape, F32)
    for i in range(4):
        a = -lift[:, i, :]
        lift_f[i * FP : i * FP + FB, :] = a
        for h in range(3):
            turned = lax.dot_general(rotate[h], a, (((0,), (0,)), ((), ())), precision=HIGH, preferred_element_type=F32)
            rot_f[h * 96 + i * FP : h * 96 + i * FP + FB, :] = turned
    lo_hi, lo_lo = halves(lift_f[...].T)
    lift_own[0] = lo_hi
    lift_own[1] = lo_lo
    lr_hi, lr_lo = halves(rot_f[...].T)
    lift_rot[0:NB] = lr_hi
    lift_rot[NB : 2 * NB] = lr_lo
    first = first.ready()
    for p in range(NF):
        put_rhs(rhs, field(p), first[:, field(p)])
    flux_own, star, dof = flux_own.ready(), star.ready(), dof.ready()
    lhs_out[...] = lhs.ready()[...]
    weights.flush()
    state[NB : 2 * NB, :] = first[...]
    state[2 * NB : 3 * NB, :] = second.ready()[...]
    for p in range(NF):
        state[3 * NB : 4 * NB, field(p)] = dof[p]

    def put(p, block):
        state[0:NB, field(p)] = dof[p] + block

    own_terms(both, rhs, moved, star, flux_own, lift_own, solved, put)
    projected[...] = moved[3 * NB :, :]


def k_pick_a(nbr, across, projected, rot, cluster, send, chosen, hot_own, hot_ghost, marks, table, table_f):
    marks.ref[0:4, :] = rot.ready()[...]
    marks.ref[4:5, :] = cluster.ready()[...]
    marks.ref[5:6, :] = send_slots(send.ready())
    nbr, across = nbr.ready(), across.ready()
    chosen, hot_own_out, hot_ghost_out = chosen.ref, hot_own, hot_ghost
    hot_own, hot_ghost = hot_own.ref, hot_ghost.ref
    rows = lax.broadcasted_iota(jnp.int32, (EL, EL), 0)
    for i in range(4):
        n = nbr[pl.ds(i, 1), :]
        key = across[pl.ds(i, 1), :] * EL + jnp.where(n < EL, n, n + (3 * EL))
        for j in range(4):
            hot_own[j * EL : (j + 1) * EL, field(i)] = jnp.where(rows + j * EL == key, 1.0, 0.0).astype(BF16)
            hot_ghost[j * EL : (j + 1) * EL, field(i)] = jnp.where(rows + (j + 4) * EL == key, 1.0, 0.0).astype(BF16)
    hot_own_out.flush()
    hot_ghost_out.flush()
    projected = projected.ready()
    gather_table(lambda j, q: projected[j * FP : (j + 1) * FP, field(q)], table, table_f)
    chosen[...] = gather_from(table, hot_own[...])


def k_own_b(own, weights, flux_own, lift_own, star, part, later, base, rhs, moved, solved):
    own, base = own.ready(), base.ref
    for p in range(NF):
        put_rhs(rhs, field(p), own[:, field(p)])
    both = weight_parts(weights.ready())[0]
    flux_own, lift_own, star, part = flux_own.ready(), lift_own.ready(), star.ready(), part.ready()

    def put(p, block):
        base[:, field(p)] = part[:, field(p)] + block

    own_terms(both, rhs, moved, star, flux_own, lift_own, solved, put)


def k_pick_b(later, weights, hot_own, base, chosen, rhs, proj_b, table, table_f):
    later, chosen = later.ready(), chosen.ref
    for p in range(NF):
        put_rhs(rhs, field(p), later[:, field(p)])
    both = weight_parts(weights.ready())[0]
    for group in PAIRS:
        cols = pair_cols(group)
        proj_b[:, cols] = dot32(both[3 * NB :, :], rhs[:, cols])
    gather_table(lambda j, q: proj_b[j * FP : (j + 1) * FP, field(q)], table, table_f)
    hot_own = hot_own.ready()
    chosen[...] = gather_from(table, hot_own[...])


def near_terms(recv, chosen, hot_ghost, weights, flux_across, marks,
               ghost, ghost_t, rhs, proj_g, table, table_f, near, solved, turned, settle, put):
    core = lax.axis_index("dom") % 2
    pos = lax.axis_index("sub")
    recv = recv.ready()
    for s in range(4):
        keep = jnp.where(pos == s, 0.0, 1.0).astype(F32)
        ghost[(4 + s) * 8 : (5 + s) * 8, :] = recv[core * 4 + s, 0] * keep
        row = pl.multiple_of(8 * ((2 - 2 * core) * 4 + s), 8)
        ghost[pl.ds(row, 8), :] = recv[(1 - core) * 4 + s, 0]
        row = pl.multiple_of(8 * (2 * core * 4 + s), 8)
        ghost[pl.ds(row, 8), :] = recv[core * 4 + s, 1]
    ghost[96:EL, :] = jnp.zeros((EL - 96, 512), F32)
    ghost_t[...] = ghost[...].T
    for q in range(NF):
        put_rhs(rhs, field(q), ghost_t[q * NB : (q + 1) * NB, :])
    both, _, lift_rot = weight_parts(weights.ready())
    for group in PAIRS:
        cols = pair_cols(group)
        proj_g[:, cols] = dot32(both[3 * NB :, :], rhs[:, cols])
    gather_table(lambda j, q: proj_g[j * FP : (j + 1) * FP, field(q)], table, table_f)
    hot_ghost, chosen = hot_ghost.ready(), chosen.ready()
    flux_across, rot = flux_across.ready(), marks.ready()
    settle()
    near[...] = chosen[...] + gather_from(table, hot_ghost[...])
    for p in range(NF):
        for i in range(4):
            s = face_mix(lambda q: near[q * FP : (q + 1) * FP, field(i)], flux_across, i, p, EL)
            solved[i * FP : (i + 1) * FP, field(p)] = s
    masks = []
    for h in range(3):
        m = [jnp.broadcast_to(jnp.where(rot[pl.ds(i, 1), :] == h, 1.0, 0.0), (FP, EL)) for i in range(4)]
        masks.append(jnp.concatenate(m, axis=0).astype(BF16))
    for group in PAIRS:
        for p in group:
            hi, lo = halves(solved[:, field(p)])
            for h in range(3):
                turned[0, h * 96 : (h + 1) * 96, field(p)] = hi * masks[h]
                turned[1, h * 96 : (h + 1) * 96, field(p)] = lo * masks[h]
        cols = pair_cols(group)
        top = dot32(lift_rot[...], turned[0, :, cols])
        put(group, top[0:NB] + top[NB : 2 * NB] + dot32(lift_rot[0:NB, :], turned[1, :, cols]))


def k_middle(recv, weights, hot_ghost, chosen, flux_across, marks, state, star,
             later, own, part, other, main,
             ghost, ghost_t, rhs, proj_g, table, table_f, near, solved, turned, moved, total, gat, res):
    box = {}
    later_out, own_out, part_out = later, own, part
    later, own, part = later.ref, own.ref, part.ref

    def settle():
        box["state"] = state.ready()
        box["fine"] = marks.ready()[4:5, :] == 0

    def put(group, block):
        for n, p in enumerate(group):
            b = block[:, n * EL : (n + 1) * EL]
            stepped = box["state"][0:NB, field(p)] + b
            part[:, field(p)] = jnp.where(box["fine"], stepped, box["state"][3 * NB : 4 * NB, field(p)] + b)
            total[:, field(p)] = stepped
            put_rhs(rhs, field(p), stepped)

    near_terms(recv, chosen, hot_ghost, weights, flux_across, marks,
               ghost, ghost_t, rhs, proj_g, table, table_f, near, solved, turned, settle, put)
    part_out.flush()
    fine = box["fine"]
    star, state = star.ready(), state.ready()
    lhs = weight_parts(weights.ready())[1]

    def add(order, p, block):
        scale = 1.0 / math.factorial(order + 1)
        t = total[:, field(p)] + scale * block
        if order < ORDER - 1:
            total[:, field(p)] = t
        else:
            sec = state[2 * NB : 3 * NB, field(p)]
            later[:, field(p)] = jnp.where(fine, t, sec)
            own[:, field(p)] = jnp.where(fine, t, state[NB : 2 * NB, field(p)] + sec)

    run_series(lhs, rhs, moved, star, add)
    later_out.flush()
    own_out.flush()
    pack_blocks(marks.ready()[5:6, :], later, gat, res, ghost, other.ref, main.ref)


def k_final(recv, weights, hot_ghost, chosen, flux_across, marks, base, out,
            ghost, ghost_t, rhs, proj_g, table, table_f, near, solved, turned):
    box = {}

    def settle():
        box["base"] = base.ready()

    def put(group, block):
        for n, p in enumerate(group):
            out.ref[p] = box["base"][:, field(p)] + block[:, n * EL : (n + 1) * EL]

    near_terms(recv, chosen, hot_ghost, weights, flux_across, marks,
               ghost, ghost_t, rhs, proj_g, table, table_f, near, solved, turned, settle, put)


class Held:
    def __init__(self, source, ref, sem):
        self.ref = ref
        self.copy = pltpu.make_async_copy(source, ref, sem)
        self.waited = False
        self.copy.start()

    def ready(self):
        if not self.waited:
            self.copy.wait()
            self.waited = True
        return self.ref


class Result:
    def __init__(self, target, ref, sem):
        self.ref = ref
        self.copy = pltpu.make_async_copy(ref, target, sem)
        self.flushed = False

    def flush(self):
        if not self.flushed:
            self.copy.start()
            self.flushed = True


class Direct:
    def __init__(self, ref):
        self.ref = ref

    def ready(self):
        return self.ref

    def flush(self):
        pass


def call_direct(kernel, name, outs, scratch, *args):
    n, m = len(args), len(outs)

    def body(*refs):
        kernel(*[Direct(r) for r in refs[: n + m]], *refs[n + m :])

    return pl.pallas_call(
        body,
        out_shape=[jax.ShapeDtypeStruct(s, d) for s, d in outs],
        in_specs=[pl.BlockSpec(memory_space=pltpu.VMEM) for _ in args],
        out_specs=[pl.BlockSpec(memory_space=pltpu.VMEM) for _ in outs],
        scratch_shapes=[pltpu.VMEM(s, d) for s, d in scratch],
        compiler_params=pltpu.CompilerParams(vmem_limit_bytes=24 * 2**20),
        name=name,
    )(*args)


def call(kernel, name, outs, scratch, *args):
    n, m = len(args), len(outs)

    def body(*refs):
        sems_in, sems_out = refs[-2:]
        held = refs[n + m : 2 * (n + m)]
        ins = [Held(refs[k], held[k], sems_in.at[k]) for k in range(n)]
        results = [Result(refs[n + k], held[n + k], sems_out.at[k]) for k in range(m)]
        kernel(*ins, *results, *refs[2 * (n + m) : -2])
        for r in results:
            r.flush()
        for a in ins:
            a.ready()
        for r in results:
            r.copy.wait()

    buffers = [pltpu.VMEM(a.shape, a.dtype) for a in args] + [pltpu.VMEM(s, d) for s, d in outs]
    return pl.pallas_call(
        body,
        out_shape=[jax.ShapeDtypeStruct(s, d) for s, d in outs],
        in_specs=[pl.BlockSpec(memory_space=pl.ANY) for _ in args],
        out_specs=[pl.BlockSpec(memory_space=pl.ANY) for _ in outs],
        scratch_shapes=[*buffers, *[pltpu.VMEM(s, d) for s, d in scratch],
                        pltpu.SemaphoreType.DMA((n,)), pltpu.SemaphoreType.DMA((m,))],
        name=name,
    )(*args)


def exchange_start(other, slabs):
    pairs = []
    for a in range(1, slabs - 1, 2):
        for s in range(4):
            pairs += [(a * 4 + s, (a + 1) * 4 + s), ((a + 1) * 4 + s, a * 4 + s)]
    return lax.ppermute(other, AXES, pairs)


def exchange_end(relay, main, slabs):
    groups = [[(2 * c + b) * 4 + s for b in range(2) for s in range(4)] for c in range(slabs // 2)]
    message = jnp.stack([main, jnp.concatenate([relay, relay], axis=0)], axis=1)
    return lax.all_to_all(message, AXES, 0, 0, axis_index_groups=groups)


def local(dof_state, stiffness, face_proj, face_lift, face_rotate, jacobians, material, inv_jacobian,
          flux_own, flux_across, cluster, neighbour, across_face, rotation, send_list):
    slabs = lax.axis_size("dom")
    dof = jnp.transpose(dof_state, (1, 0, 2))
    jac = jnp.transpose(jacobians, (2, 3, 1, 0)).reshape(81, 3, 16)
    proj = jnp.transpose(face_proj, (1, 0, 2))
    lift = jnp.transpose(face_lift, (2, 0, 1))
    f_own = jnp.transpose(flux_own, (1, 2, 0, 3)).reshape(81, 4, EL)
    f_across = jnp.transpose(flux_across, (1, 2, 0, 3)).reshape(81, 4, EL)
    mat = material.reshape(1, EL)
    clu = cluster.reshape(1, EL)
    send = send_list.reshape(1, 96)
    state = ((NB, WID), F32)
    blocks = [((4, 8, 512), F32), ((8, 8, 512), F32)]
    rhs = ((192, WID), BF16)
    pack = [((576, 2 * EL), BF16), ((512, EL), F32), ((EL, 512), F32)]
    star, first, second, other, main, lhs = call(
        k_predict, "predict",
        [((243, EL), F32), state, state, *blocks, ((168, 192), BF16)],
        [((168, 192), BF16), rhs, ((2, 168, WID), F32), *pack],
        mat, jac, inv_jacobian, stiffness, dof, send)
    relay = exchange_start(other, slabs)
    rows = ((224, 512), F32)
    hot = ((512, 512), BF16)
    tables = [((448, 512), BF16), rows]
    own_scratch = [rhs, ((264, WID), F32), ((96, WID), F32)]
    state_pack, projected, weights, lift_own = call(
        k_own_a, "own_a",
        [((4 * NB, WID), F32), ((96, WID), F32), ((544, 288), BF16), ((2, NB, 96), BF16)],
        [*own_scratch, ((96, NB), F32), ((288, NB), F32)],
        stiffness, proj, lift, face_rotate, first, f_own, star, dof, lhs, second)
    relay, projected = lax.optimization_barrier((relay, projected))
    chosen, hot_own, hot_ghost, marks = call_direct(
        k_pick_a, "pick_a", [rows, hot, hot, ((8, EL), jnp.int32)], tables,
        neighbour, across_face, projected, rotation, clu, send)
    recv = exchange_end(relay, main, slabs)
    near_scratch = [((EL, 512), F32), ((512, EL), F32), rhs, ((96, WID), F32), *tables, rows, ((96, WID), F32), ((2, 288, WID), BF16)]
    later, own, part, other, main = call_direct(
        k_middle, "middle", [state, state, state, *blocks],
        [*near_scratch, ((2, 168, WID), F32), state, pack[0], pack[1]],
        recv, weights, hot_ghost, chosen, f_across, marks, state_pack, star)
    relay = exchange_start(other, slabs)
    (base,) = call_direct(k_own_b, "own_b", [state], own_scratch, own, weights, f_own, lift_own, star, part, later)
    relay, base, later = lax.optimization_barrier((relay, base, later))
    (chosen,) = call_direct(k_pick_b, "pick_b", [rows], [rhs, ((96, WID), F32), *tables], later, weights, hot_own, base)
    recv = exchange_end(relay, main, slabs)
    (out,) = call_direct(
        k_final, "final", [((NF, NB, EL), F32)], near_scratch,
        recv, weights, hot_ghost, chosen, f_across, marks, base)
    return jnp.transpose(out, (1, 0, 2))


def solution(mesh):
    both = ("dom", "sub")
    in_specs = (
        P(None, None, both), P(), P(), P(), P(), P(), P(both), P(None, None, both),
        P(None, None, None, both), P(None, None, None, both), P(both), P(None, both),
        P(None, both), P(None, both), P(both),
    )
    return jax.shard_map(local, mesh=mesh, in_specs=in_specs, out_specs=P(None, None, both), check_vma=False)
```
